32 devices in a mesh: group: 2 (over y), expert: 4 (over z), dp: 4 (over x, core).
Axes of the slice: x: 2, y: 2, z: 4, core: 2. Of those that a mesh axis runs over, the one named last changes fastest.
Arguments:
- tokens: bfloat16 [256, 4096], P(('group', 'expert', 'dp')), parts along dimension 0, may hold values from -6 to 6
- routing: int32 [256, 8], P(('group', 'expert', 'dp')), parts along dimension 0, may hold values from 0 to 127, as said below
- gate_quantized: int32 [256, 8], P(('group', 'expert', 'dp')), parts along dimension 0, may hold values from 1 to 32767
- tenant: int32 [256], P(('group', 'expert', 'dp')), parts along dimension 0, may hold values from 0 to 23
- tenant_page_lookup: int32 [4, 24], replicated, may hold values from 0 to 23, each once within a row
- gate_weight: bfloat16 [4, 4096, 1024], P('expert', None, 'dp'), may hold values from -0.09375 to 0.09375
- up_projection: bfloat16 [4, 4096, 1024], P('expert', None, 'dp'), may hold values from -0.09375 to 0.09375
- down_weight: bfloat16 [4, 1024, 4096], P('expert', None, 'dp'), may hold values from -0.1875 to 0.1875
- adapter_shrink: bfloat16 [4, 24, 16, 4096], P('expert', 'dp'), may hold values from -0.09375 to 0.09375
- adapter_expand: bfloat16 [4, 24, 16, 1024], P('expert', 'dp'), may hold values from -1.5 to 1.5
Outputs:
- mixed_out: bfloat16 [256, 4096], P(('group', 'expert', 'dp')), parts along dimension 0
The draws below stay inside these ranges and needn't reach their ends.
There are 2 independent parts, one for each index of `group`. The reference program is written for one: setup_inputs(seed, part) draws one part's arguments, and reference() takes and returns one part's arrays. A program takes and returns all parts, laid end to end along the dimension named above; an argument that names none is the same for every part. Nothing has to cross between parts.
Inputs may be any that keep to these rules, and one draw needn't show every extreme that they name: `routing`: each row names 8 different experts. Among the 8 tokens of one device no expert is named more than 2 times, and in every draw some expert below 4 is named exactly 2 times by the tokens of every device. `tenant_page_lookup`: row e gives every tenant a different page of expert e's pool.
All inputs are finite; a program needn't handle non-finite values.
Results may differ from the reference program's by a relative error of at most 0.0061.
Values may be sent and summed in bfloat16 or wider, within the bound.
A program may use at most 64 MiB of HBM per device.

```python
import jax
import jax.numpy as jnp
from jax import lax

MODEL_DIMENSION = 4096
EXPERT_HIDDEN = 1024
EXPERTS_ALL = 128
TOPK = 8
ADAPTER_RANK = 16
TENANT_COUNT = 24
TOK_DEV = 8
FLIGHT_EXPERTS = 4
TOKENS = 128
N_EXPERT = 4
N_DP = 4


def draw_routing(key, part):
    unit = TOK_DEV // 8
    loaded_base = jnp.concatenate([jnp.full((16,), 2 * unit, jnp.int32), jnp.full((32,), unit, jnp.int32)])
    hottest = jax.random.randint(jax.random.fold_in(key, 11), (), 0, FLIGHT_EXPERTS)
    block_total = TOKENS // TOK_DEV
    places = jnp.arange(TOK_DEV * TOPK, dtype=jnp.int32)
    all_ids = jnp.arange(EXPERTS_ALL, dtype=jnp.int32)

    def one_block(block_key):
        first_key, second_key, third_key = jax.random.split(block_key, 3)
        shuffled_ids = jax.random.permutation(first_key, EXPERTS_ALL).astype(jnp.int32)
        order_key = jnp.where(shuffled_ids < FLIGHT_EXPERTS, 0, EXPERTS_ALL).astype(jnp.int32) + all_ids
        ordered_ids = shuffled_ids[jnp.argsort(order_key, stable=True)]
        loaded = loaded_base[jax.random.permutation(third_key, 48)]
        loaded_full = jnp.concatenate([loaded, jnp.zeros((EXPERTS_ALL - 48,), jnp.int32)])
        loads = jnp.zeros((EXPERTS_ALL,), jnp.int32).at[ordered_ids].set(loaded_full)
        where_full = jnp.argmax((loads == 2 * unit).astype(jnp.int32))
        loads = loads.at[where_full].set(loads[hottest]).at[hottest].set(2 * unit)
        ends = jnp.cumsum(loads)
        listed = jnp.sum((ends[None, :] <= places[:, None]).astype(jnp.int32), axis=1)
        chosen = listed.reshape(TOPK, TOK_DEV).T
        shuffle = jax.random.permutation(second_key, TOK_DEV)
        return chosen[shuffle]
    block_keys = jax.random.split(jax.random.fold_in(key, 5), block_total)
    return jax.vmap(one_block)(block_keys).reshape(TOKENS, TOPK).astype(jnp.int32)


def set_ends(entries, own_key, least, high):
    extent = entries.shape
    spot = [jax.random.randint(jax.random.fold_in(own_key, axis), (), 0, extent[axis]) for axis in range(len(extent))]
    entries = entries.at[tuple(spot)].set(least)
    longest = extent.index(max(extent))
    spot[longest] = (spot[longest] + 1) % extent[longest]
    return entries.at[tuple(spot)].set(high)


def steps_of(rng, dims, cuts, smallest, high):
    factor_of = 1.0
    for dim, shards_of in cuts:
        draws = jax.random.uniform(jax.random.fold_in(jax.random.fold_in(rng, 6), dim), (shards_of,), jnp.float32, smallest / len(cuts), high / len(cuts))
        factor_of = factor_of * jnp.repeat(jnp.exp(draws), dims[dim] // shards_of).reshape((-1,) + (1,) * (len(dims) - 1 - dim))
    return factor_of


def scatter_about(key, extent, deviation, reach, shards=(), held_as=jnp.bfloat16):
    values = deviation * jax.random.normal(key, extent, jnp.float32)
    if shards:
        values = values * steps_of(key, extent, shards, -0.22, 0.18)
    return jnp.clip(values, -reach, reach).astype(held_as)


def setup_inputs(seed: int = 0, part: int = 0) -> dict:
    seeds = jax.random.split(jax.random.key(seed), 11)
    part_keys = jax.random.split(jax.random.fold_in(seeds[10], part), 11)
    return {
        "tokens": scatter_about(part_keys[0], (TOKENS, MODEL_DIMENSION), 1.0, 6.0, ((0, 16),)),
        "routing": draw_routing(jax.random.fold_in(jax.random.fold_in(seeds[10], part), 71), part),
        "gate_quantized": set_ends(jax.random.randint(part_keys[2], (TOKENS, TOPK), 1, 32768), jax.random.fold_in(part_keys[2], 1), 1, 32767).astype(jnp.int32),
        "tenant": set_ends(jax.random.randint(part_keys[3], (TOKENS,), 0, TENANT_COUNT), jax.random.fold_in(part_keys[3], 1), 0, TENANT_COUNT - 1).astype(jnp.int32),
        "tenant_page_lookup": jax.vmap(lambda own: jax.random.permutation(own, TENANT_COUNT))(jax.random.split(seeds[4], FLIGHT_EXPERTS)).reshape((FLIGHT_EXPERTS, TENANT_COUNT)).astype(jnp.int32),
        "gate_weight": scatter_about(seeds[5], (FLIGHT_EXPERTS, MODEL_DIMENSION, EXPERT_HIDDEN), MODEL_DIMENSION ** -0.5, 0.09375, ((0, 4), (2, 4))),
        "up_projection": scatter_about(seeds[6], (FLIGHT_EXPERTS, MODEL_DIMENSION, EXPERT_HIDDEN), MODEL_DIMENSION ** -0.5, 0.09375, ((0, 4), (2, 4))),
        "down_weight": scatter_about(seeds[7], (FLIGHT_EXPERTS, EXPERT_HIDDEN, MODEL_DIMENSION), EXPERT_HIDDEN ** -0.5, 0.1875, ((0, 4), (2, 4))),
        "adapter_shrink": scatter_about(seeds[8], (FLIGHT_EXPERTS, TENANT_COUNT, ADAPTER_RANK, MODEL_DIMENSION), MODEL_DIMENSION ** -0.5, 0.09375, ((0, 4), (1, 4))),
        "adapter_expand": scatter_about(seeds[9], (FLIGHT_EXPERTS, TENANT_COUNT, ADAPTER_RANK, EXPERT_HIDDEN), ADAPTER_RANK ** -0.5, 1.5, ((0, 4), (1, 4))),
    }


def reference(tokens, routing, gate_quantized, tenant, tenant_page_lookup, gate_weight, up_projection, down_weight, adapter_shrink, adapter_expand):
    devices_all = N_EXPERT * N_DP
    capacity = TOK_DEV // 4
    slot_total = devices_all * capacity
    expert_ids = jnp.arange(FLIGHT_EXPERTS, dtype=jnp.int32)
    matches = routing[:, :, None] == expert_ids[None, None, :]
    assign = jnp.sum(matches.astype(jnp.int32), axis=1)
    mix_coef = jnp.sum(jnp.where(matches, gate_quantized[:, :, None].astype(jnp.float32) / 32768.0, jnp.float32(0.0)), axis=1)
    blocked = assign.reshape(devices_all, TOK_DEV, FLIGHT_EXPERTS)
    slot_rank = (jnp.cumsum(blocked, axis=1) - blocked).reshape(TOKENS, FLIGHT_EXPERTS)
    token_ids = jnp.arange(TOKENS, dtype=jnp.int32)
    source = token_ids // TOK_DEV
    slot_of = jnp.where(assign == 1, source[:, None] * capacity + slot_rank, slot_total).astype(jnp.int32)

    def one_expert(running, expert_number):
        slot_here = lax.dynamic_index_in_dim(slot_of, expert_number, 1, keepdims=False)
        holder = jnp.full((slot_total,), TOKENS, jnp.int32).at[slot_here].set(token_ids, mode="drop")
        occupied = holder < TOKENS
        safe_ids = jnp.minimum(holder, TOKENS - 1).astype(jnp.int32)
        slot_input = jnp.where(occupied[:, None], tokens[safe_ids], jnp.zeros((), tokens.dtype))
        page_row = lax.dynamic_index_in_dim(tenant_page_lookup, expert_number, 0, keepdims=False)
        page_numbers = page_row[tenant[safe_ids]].astype(jnp.int32)
        shrink_weight = lax.dynamic_index_in_dim(adapter_shrink, expert_number, 0, keepdims=False)
        products = jnp.dot(slot_input, shrink_weight.reshape(TENANT_COUNT * ADAPTER_RANK, MODEL_DIMENSION).T, preferred_element_type=jnp.float32)
        products = products.reshape(slot_total, TENANT_COUNT, ADAPTER_RANK)
        shrink_result = jnp.take_along_axis(products, page_numbers[:, None, None], axis=1)[:, 0, :].astype(jnp.bfloat16)
        expand_weight = lax.dynamic_index_in_dim(adapter_expand, expert_number, 0, keepdims=False)[page_numbers]
        adapter_update = jnp.einsum("cz,czy->cy", shrink_result.astype(jnp.float32), expand_weight.astype(jnp.float32))
        gate_w = lax.dynamic_index_in_dim(gate_weight, expert_number, 0, keepdims=False)
        up_weight = lax.dynamic_index_in_dim(up_projection, expert_number, 0, keepdims=False)
        down_w = lax.dynamic_index_in_dim(down_weight, expert_number, 0, keepdims=False)
        gate_act = jnp.dot(slot_input, gate_w, preferred_element_type=jnp.float32)
        up_activation = jnp.dot(slot_input, up_weight, preferred_element_type=jnp.float32) + adapter_update
        hidden = (jax.nn.silu(gate_act) * up_activation).astype(jnp.bfloat16)
        expert_out = jnp.dot(hidden, down_w, preferred_element_type=jnp.float32).astype(jnp.bfloat16)
        coef_here = lax.dynamic_index_in_dim(mix_coef, expert_number, 1, keepdims=False)[safe_ids]
        weight_here = jnp.where(occupied, coef_here, jnp.float32(0.0))
        running = running.at[safe_ids].add(weight_here[:, None] * expert_out.astype(jnp.float32))
        return running, None

    mixed_out, unused = lax.scan(one_expert, jnp.zeros((TOKENS, MODEL_DIMENSION), jnp.float32), expert_ids)
    return mixed_out.astype(jnp.bfloat16)
```

```python
import functools

import jax
import jax.numpy as jnp
from jax import lax
from jax.experimental import pallas as pl
from jax.experimental.pallas import tpu as pltpu
from jax.sharding import PartitionSpec as P

MESH = pl.DeviceIdType.MESH
F32 = jnp.float32
BF16 = jnp.bfloat16


def iota(shape, dim):
    return lax.broadcasted_iota(jnp.int32, shape, dim)


def dot(a, b):
    return jnp.dot(a, b, preferred_element_type=F32)


def dot_nt(a, b):
    return lax.dot_general(a, b, (((1,), (1,)), ((), ())), preferred_element_type=F32)


def kernel(
    n_e,
    n_dp,
    tok,
    rout,
    gq,
    ten,
    look,
    gw,
    uw,
    dw,
    shr,
    exp,
    out,
    send,
    rows,
    spread,
    expand,
    hid,
    eout,
    back,
    gw_v,
    uw_v,
    dw_v,
    shr_v,
    load_sem,
    z_send,
    row_recv,
    f_send,
    x_send,
    x_recv,
    s_send,
    s_recv,
    h_send,
    h_recv,
    o_send,
    o_recv,
):
    e_me = lax.axis_index("expert")
    d_me = lax.axis_index("dp")
    tokens, width = tok.shape
    experts, tenants = look.shape
    topk = rout.shape[1]
    cap = send.shape[1]
    slots_out = experts * cap
    wide = send.shape[2]
    pages, rank_dim = shr_v.shape[:2]
    hidden_part = gw_v.shape[1]
    out_part = dw_v.shape[1]
    pr = pages * rank_dim

    barrier = pltpu.get_barrier_semaphore()
    for i in range(1, n_e):
        pl.semaphore_signal(
            barrier, inc=1, device_id={"expert": lax.rem(e_me + i, n_e)}, device_id_type=MESH
        )
    for i in range(1, n_dp):
        pl.semaphore_signal(
            barrier, inc=1, device_id={"dp": lax.rem(d_me + i, n_dp)}, device_id_type=MESH
        )

    loads = [
        pltpu.make_async_copy(shr.at[0], shr_v, load_sem.at[0]),
        pltpu.make_async_copy(gw.at[0], gw_v, load_sem.at[1]),
        pltpu.make_async_copy(uw.at[0], uw_v, load_sem.at[2]),
        pltpu.make_async_copy(
            exp.at[0, :, :, pl.ds(pl.multiple_of(d_me * hidden_part, hidden_part), hidden_part)],
            expand.at[d_me],
            load_sem.at[3],
        ),
        pltpu.make_async_copy(dw.at[0], dw_v, load_sem.at[4]),
    ]
    for c in loads:
        c.start()

    routing = rout[...]
    routing_f = routing.astype(F32)
    eye = (iota((topk, topk), 0) == iota((topk, topk), 1)).astype(F32)
    routing_t = dot_nt(eye, routing_f)
    j_row = iota((slots_out, tokens), 0)
    e_row = (j_row // cap).astype(F32)
    assign_t = jnp.zeros((slots_out, tokens), F32)
    for k in range(topk):
        assign_t += (routing_t[k : k + 1, :] == e_row).astype(F32)
    upper = (iota((tokens, tokens), 0) < iota((tokens, tokens), 1)).astype(F32)
    rank_t = dot(assign_t, upper)
    place_t = assign_t * (rank_t == lax.rem(j_row, cap).astype(F32)).astype(F32)
    x_out = dot(place_t.astype(BF16), tok[...])
    ten_row = iota((tokens, tenants), 0)
    ten_col = jnp.zeros((tokens, tenants), jnp.int32)
    for t in range(tokens):
        ten_col = jnp.where(ten_row == t, ten[t], ten_col)
    ten_hot = (ten_col == iota((tokens, tenants), 1)).astype(F32)
    slot_ten = dot(place_t, ten_hot)
    pick_e = (iota((slots_out, experts), 0) // cap == iota((slots_out, experts), 1)).astype(F32)
    look_rows = dot(pick_e, look[...].astype(F32))
    page = jnp.sum(slot_ten * look_rows, axis=1, keepdims=True)
    filled = jnp.sum(slot_ten, axis=1, keepdims=True)
    tail = wide - width
    page_hot = (page == iota((slots_out, tail), 1).astype(F32)).astype(F32) * filled
    for e in range(experts):
        send[e, :, :width] = x_out[e * cap : (e + 1) * cap, :].astype(BF16)
        send[e, :, width:] = page_hot[e * cap : (e + 1) * cap, :].astype(BF16)
    rows[e_me, d_me] = send[e_me]

    pl.semaphore_wait(barrier, n_e - 1 + n_dp - 1)

    waits = []
    order = sorted(range(1, n_e), key=lambda i: -min(i, n_e - i))
    for i in order:
        e = lax.rem(e_me + i, n_e)
        c = pltpu.make_async_remote_copy(
            src_ref=send.at[e],
            dst_ref=rows.at[e_me, d_me],
            send_sem=z_send.at[i],
            recv_sem=row_recv.at[e_me, d_me],
            device_id={"expert": e},
            device_id_type=MESH,
        )
        c.start()
        waits.append(c)

    def forward(z, slot):
        for i in range(1, n_dp):
            c = pltpu.make_async_remote_copy(
                src_ref=rows.at[z, d_me],
                dst_ref=rows.at[z, d_me],
                send_sem=f_send.at[slot, i],
                recv_sem=row_recv.at[z, d_me],
                device_id={"dp": lax.rem(d_me + i, n_dp)},
                device_id_type=MESH,
            )
            c.start()
            waits.append(c)

    def row_wait(z, d):
        pltpu.make_async_copy(rows.at[z, d], rows.at[z, d], row_recv.at[z, d]).wait()

    forward(e_me, 0)
    for i in range(1, n_dp):
        d = lax.rem(d_me + i, n_dp)
        c = pltpu.make_async_remote_copy(
            src_ref=exp.at[
                0, :, :, pl.ds(pl.multiple_of(d * hidden_part, hidden_part), hidden_part)
            ],
            dst_ref=expand.at[d_me],
            send_sem=x_send.at[i],
            recv_sem=x_recv.at[d_me],
            device_id={"dp": d},
            device_id_type=MESH,
        )
        c.start()
        waits.append(c)
    for i in sorted(range(1, n_e), key=lambda i: min(i, n_e - i)):
        z = lax.rem(e_me + i, n_e)
        row_wait(z, d_me)
        forward(z, i)
    for i in range(1, n_dp):
        for z in range(n_e):
            row_wait(z, lax.rem(d_me + i, n_dp))

    slot_count = n_e * n_dp * cap
    x_all = rows[...].astype(F32).reshape(slot_count, wide).astype(BF16)
    x_in = x_all[:, :width]
    hot = x_all[:, width:]
    loads[0].wait()
    products = dot_nt(x_in, shr_v[...].reshape(pr, width))
    own_pages = (
        iota((tail, pr), 0) == d_me * pages + iota((tail, pr), 1) // rank_dim
    ).astype(BF16)
    mask = dot(hot, own_pages)
    pad = spread.shape[2] - pr
    low = products.astype(BF16).astype(F32) * mask
    if pad:
        low = jnp.concatenate([low, jnp.zeros((slot_count, pad), F32)], axis=1)
    spread[d_me] = low.astype(BF16)
    for i in range(1, n_dp):
        c = pltpu.make_async_remote_copy(
            src_ref=spread.at[d_me],
            dst_ref=spread.at[d_me],
            send_sem=s_send.at[i],
            recv_sem=s_recv.at[d_me],
            device_id={"dp": lax.rem(d_me + i, n_dp)},
            device_id_type=MESH,
        )
        c.start()
        waits.append(c)

    loads[1].wait()
    gate_act = dot(x_in, gw_v[...])
    loads[2].wait()
    up_act = dot(x_in, uw_v[...])
    loads[3].wait()
    for i in range(n_dp):
        d = lax.rem(d_me + i, n_dp)
        if i:
            pltpu.make_async_copy(spread.at[d], spread.at[d], s_recv.at[d]).wait()
            pltpu.make_async_copy(expand.at[d], expand.at[d], x_recv.at[d]).wait()
        up_act += dot(spread[d][:, :pr], expand[d].reshape(pr, hidden_part))
    hidden = (gate_act / (1.0 + jnp.exp(-gate_act))) * up_act
    hid[d_me] = hidden.astype(BF16)
    for i in range(1, n_dp):
        c = pltpu.make_async_remote_copy(
            src_ref=hid.at[d_me],
            dst_ref=hid.at[d_me],
            send_sem=h_send.at[i],
            recv_sem=h_recv.at[d_me],
            device_id={"dp": lax.rem(d_me + i, n_dp)},
            device_id_type=MESH,
        )
        c.start()
        waits.append(c)

    j_col = iota((tokens, slots_out), 1)
    e_col = j_col // cap
    quant = gq[...]
    high = lax.shift_right_logical(quant, 8)
    rest = quant - high * 256
    assign = jnp.zeros((tokens, slots_out), F32)
    mix_high = jnp.zeros((tokens, slots_out), F32)
    mix_rest = jnp.zeros((tokens, slots_out), F32)
    for k in range(topk):
        hit = (routing[:, k : k + 1] == e_col).astype(F32)
        assign += hit
        mix_high += hit * (high[:, k : k + 1].astype(F32) * (256.0 / 32768.0))
        mix_rest += hit * (rest[:, k : k + 1].astype(F32) * (1.0 / 32768.0))
    lower = (iota((tokens, tokens), 1) < iota((tokens, tokens), 0)).astype(F32)
    rank = dot(lower, assign)
    here = (rank == lax.rem(j_col, cap).astype(F32)).astype(F32)
    mix = jnp.concatenate([mix_high * here, mix_rest * here], axis=0).astype(BF16)

    loads[4].wait()
    total = None
    for i in range(n_dp):
        d = lax.rem(d_me + i, n_dp)
        if i:
            pltpu.make_async_copy(hid.at[d], hid.at[d], h_recv.at[d]).wait()
        part = dot(
            hid[d], dw_v[pl.ds(pl.multiple_of(d * hidden_part, hidden_part), hidden_part), :]
        )
        total = part if total is None else total + part
    for z in range(n_e):
        for d in range(n_dp):
            base = (z * n_dp + d) * cap
            eout[z, d] = total[base : base + cap, :].astype(BF16)

    back[e_me, d_me] = eout[e_me, d_me]
    for i in sorted(range(n_e), key=lambda i: -min(i, n_e - i)):
        z = lax.rem(e_me + i, n_e)
        for j in range(n_dp - 1, -1, -1):
            if i == 0 and j == 0:
                continue
            d = lax.rem(d_me + j, n_dp)
            c = pltpu.make_async_remote_copy(
                src_ref=eout.at[z, d],
                dst_ref=back.at[e_me, d_me],
                send_sem=o_send.at[i, j],
                recv_sem=o_recv.at[e_me, d_me],
                device_id={"expert": z, "dp": d},
                device_id_type=MESH,
            )
            c.start()
            waits.append(c)
    for i in range(n_e):
        z = lax.rem(e_me + i, n_e)
        for j in range(n_dp):
            if i == 0 and j == 0:
                continue
            d = lax.rem(d_me + j, n_dp)
            pltpu.make_async_copy(back.at[z, d], back.at[z, d], o_recv.at[z, d]).wait()
    for d in range(n_dp):
        got = back[:, d].astype(F32).reshape(slots_out, out_part).astype(BF16)
        both = dot(mix, got)
        out[:, d * out_part : (d + 1) * out_part] = (both[:tokens] + both[tokens:]).astype(BF16)
    for c in waits:
        c.wait_send()


def per_device(n_e, n_dp, tok, rout, gq, ten, look, gw, uw, dw, shr, exp):
    tokens, width = tok.shape
    experts, tenants = look.shape
    cap = tokens // 4
    tail = -(-tenants // 128) * 128
    wide = width + tail
    pages, rank_dim = shr.shape[1:3]
    hidden_part = gw.shape[2]
    out_part = dw.shape[2]
    slot_count = n_e * n_dp * cap
    pr_pad = -(-pages * rank_dim // 128) * 128
    vmem = pl.BlockSpec(memory_space=pltpu.VMEM)
    hbm = pl.BlockSpec(memory_space=pl.ANY)
    dma = pltpu.SemaphoreType.DMA
    return pl.pallas_call(
        functools.partial(kernel, n_e, n_dp),
        out_shape=jax.ShapeDtypeStruct((tokens, width), BF16),
        in_specs=[
            vmem,
            vmem,
            vmem,
            pl.BlockSpec(memory_space=pltpu.SMEM),
            vmem,
            hbm,
            hbm,
            hbm,
            hbm,
            hbm,
        ],
        out_specs=vmem,
        scratch_shapes=[
            pltpu.VMEM((experts, cap, wide), BF16),
            pltpu.VMEM((n_e, n_dp, cap, wide), BF16),
            pltpu.VMEM((n_dp, slot_count, pr_pad), BF16),
            pltpu.VMEM((n_dp, pages, rank_dim, hidden_part), BF16),
            pltpu.VMEM((n_dp, slot_count, hidden_part), BF16),
            pltpu.VMEM((n_e, n_dp, cap, out_part), BF16),
            pltpu.VMEM((n_e, n_dp, cap, out_part), BF16),
            pltpu.VMEM(gw.shape[1:], BF16),
            pltpu.VMEM(uw.shape[1:], BF16),
            pltpu.VMEM(dw.shape[1:], BF16),
            pltpu.VMEM(shr.shape[1:], BF16),
            dma((5,)),
            dma((n_e,)),
            dma((n_e, n_dp)),
            dma((n_e, n_dp)),
            dma((n_dp,)),
            dma((n_dp,)),
            dma((n_dp,)),
            dma((n_dp,)),
            dma((n_dp,)),
            dma((n_dp,)),
            dma((n_e, n_dp)),
            dma((n_e, n_dp)),
        ],
        compiler_params=pltpu.CompilerParams(collective_id=0, has_side_effects=True),
    )(tok, rout, gq, ten, look, gw, uw, dw, shr, exp)


def solution(mesh):
    return jax.shard_map(
        functools.partial(per_device, mesh.shape["expert"], mesh.shape["dp"]),
        mesh=mesh,
        in_specs=(
            P(("group", "expert", "dp"), None),
            P(("group", "expert", "dp"), None),
            P(("group", "expert", "dp"), None),
            P(("group", "expert", "dp")),
            P(),
            P("expert", None, "dp"),
            P("expert", None, "dp"),
            P("expert", None, "dp"),
            P("expert", "dp", None, None),
            P("expert", "dp", None, None),
        ),
        out_specs=P(("group", "expert", "dp"), None),
        check_vma=False,
    )
```

```python
import functools

import jax
import jax.numpy as jnp
from jax import lax
from jax.experimental import pallas as pl
from jax.experimental.pallas import tpu as pltpu
from jax.sharding import PartitionSpec as P

MESH = pl.DeviceIdType.MESH
F32 = jnp.float32
BF16 = jnp.bfloat16


def iota(shape, dim):
    return lax.broadcasted_iota(jnp.int32, shape, dim)


def dot(a, b):
    return jnp.dot(a, b, preferred_element_type=F32)


def dot_nt(a, b):
    return lax.dot_general(a, b, (((1,), (1,)), ((), ())), preferred_element_type=F32)


def kernel(
    n_e,
    n_dp,
    tok_h,
    rout_h,
    gq_h,
    ten_h,
    look_h,
    gw,
    uw,
    dw,
    shr,
    exp,
    out,
    send,
    rows,
    spread,
    expand,
    hid,
    eout,
    back,
    gw_v,
    uw_v,
    dw_v,
    shr_v,
    tok,
    rout,
    gq,
    ten,
    look,
    small_sem,
    load_sem,
    z_send,
    row_recv,
    f_send,
    x_send,
    x_recv,
    s_send,
    s_recv,
    h_send,
    h_recv,
    o_send,
    o_recv,
):
    e_me = lax.axis_index("expert")
    d_me = lax.axis_index("dp")
    tokens, width = tok.shape
    experts, tenants = look.shape
    topk = rout.shape[1]
    cap = send.shape[1]
    slots_out = experts * cap
    wide = send.shape[2]
    pages, rank_dim = shr_v.shape[:2]
    hidden_part = gw_v.shape[1]
    out_part = dw_v.shape[1]
    pr = pages * rank_dim

    barrier = pltpu.get_barrier_semaphore()
    for i in range(1, n_e):
        pl.semaphore_signal(
            barrier, inc=1, device_id={"expert": lax.rem(e_me + i, n_e)}, device_id_type=MESH
        )
    for i in range(1, n_dp):
        pl.semaphore_signal(
            barrier, inc=1, device_id={"dp": lax.rem(d_me + i, n_dp)}, device_id_type=MESH
        )

    small = [
        pltpu.make_async_copy(src, dst, small_sem.at[i])
        for i, (src, dst) in enumerate(
            ((rout_h, rout), (ten_h, ten), (look_h, look), (tok_h, tok), (gq_h, gq))
        )
    ]
    for c in small:
        c.start()
    loads = [
        pltpu.make_async_copy(shr.at[0], shr_v, load_sem.at[0]),
        pltpu.make_async_copy(gw.at[0], gw_v, load_sem.at[1]),
        pltpu.make_async_copy(uw.at[0], uw_v, load_sem.at[2]),
        pltpu.make_async_copy(
            exp.at[0, :, :, pl.ds(pl.multiple_of(d_me * hidden_part, hidden_part), hidden_part)],
            expand.at[d_me],
            load_sem.at[3],
        ),
        pltpu.make_async_copy(dw.at[0], dw_v, load_sem.at[4]),
    ]
    for c in loads:
        c.start()

    for c in small:
        c.wait()
    routing = rout[...]
    routing_f = routing.astype(F32)
    eye = (iota((topk, topk), 0) == iota((topk, topk), 1)).astype(F32)
    routing_t = dot_nt(eye, routing_f)
    j_row = iota((slots_out, tokens), 0)
    e_row = (j_row // cap).astype(F32)
    assign_t = jnp.zeros((slots_out, tokens), F32)
    for k in range(topk):
        assign_t += (routing_t[k : k + 1, :] == e_row).astype(F32)
    upper = (iota((tokens, tokens), 0) < iota((tokens, tokens), 1)).astype(F32)
    rank_t = dot(assign_t, upper)
    place_t = assign_t * (rank_t == lax.rem(j_row, cap).astype(F32)).astype(F32)
    x_out = dot(place_t.astype(BF16), tok[...])
    ten_row = iota((tokens, tenants), 0)
    ten_col = jnp.zeros((tokens, tenants), jnp.int32)
    for t in range(tokens):
        ten_col = jnp.where(ten_row == t, ten[t], ten_col)
    ten_hot = (ten_col == iota((tokens, tenants), 1)).astype(F32)
    slot_ten = dot(place_t, ten_hot)
    pick_e = (iota((slots_out, experts), 0) // cap == iota((slots_out, experts), 1)).astype(F32)
    look_rows = dot(pick_e, look[...].astype(F32))
    page = jnp.sum(slot_ten * look_rows, axis=1, keepdims=True)
    filled = jnp.sum(slot_ten, axis=1, keepdims=True)
    tail = wide - width
    page_hot = (page == iota((slots_out, tail), 1).astype(F32)).astype(F32) * filled
    for e in range(experts):
        send[e, :, :width] = x_out[e * cap : (e + 1) * cap, :].astype(BF16)
        send[e, :, width:] = page_hot[e * cap : (e + 1) * cap, :].astype(BF16)
    rows[e_me, d_me] = send[e_me]

    pl.semaphore_wait(barrier, n_e - 1 + n_dp - 1)

    waits = []
    order = sorted(range(1, n_e), key=lambda i: -min(i, n_e - i))
    for i in order:
        e = lax.rem(e_me + i, n_e)
        c = pltpu.make_async_remote_copy(
            src_ref=send.at[e],
            dst_ref=rows.at[e_me, d_me],
            send_sem=z_send.at[i],
            recv_sem=row_recv.at[e_me, d_me],
            device_id={"expert": e},
            device_id_type=MESH,
        )
        c.start()
        waits.append(c)

    def forward(z, slot):
        for i in range(1, n_dp):
            c = pltpu.make_async_remote_copy(
                src_ref=rows.at[z, d_me],
                dst_ref=rows.at[z, d_me],
                send_sem=f_send.at[slot, i],
                recv_sem=row_recv.at[z, d_me],
                device_id={"dp": lax.rem(d_me + i, n_dp)},
                device_id_type=MESH,
            )
            c.start()
            waits.append(c)

    def row_wait(z, d):
        pltpu.make_async_copy(rows.at[z, d], rows.at[z, d], row_recv.at[z, d]).wait()

    forward(e_me, 0)
    for i in range(1, n_dp):
        d = lax.rem(d_me + i, n_dp)
        c = pltpu.make_async_remote_copy(
            src_ref=exp.at[
                0, :, :, pl.ds(pl.multiple_of(d * hidden_part, hidden_part), hidden_part)
            ],
            dst_ref=expand.at[d_me],
            send_sem=x_send.at[i],
            recv_sem=x_recv.at[d_me],
            device_id={"dp": d},
            device_id_type=MESH,
        )
        c.start()
        waits.append(c)
    for i in sorted(range(1, n_e), key=lambda i: min(i, n_e - i)):
        z = lax.rem(e_me + i, n_e)
        row_wait(z, d_me)
        forward(z, i)
    for i in range(1, n_dp):
        for z in range(n_e):
            row_wait(z, lax.rem(d_me + i, n_dp))

    slot_count = n_e * n_dp * cap
    x_all = rows[...].astype(F32).reshape(slot_count, wide).astype(BF16)
    x_in = x_all[:, :width]
    hot = x_all[:, width:]
    loads[0].wait()
    products = dot_nt(x_in, shr_v[...].reshape(pr, width))
    own_pages = (
        iota((tail, pr), 0) == d_me * pages + iota((tail, pr), 1) // rank_dim
    ).astype(BF16)
    mask = dot(hot, own_pages)
    pad = spread.shape[2] - pr
    low = products.astype(BF16).astype(F32) * mask
    if pad:
        low = jnp.concatenate([low, jnp.zeros((slot_count, pad), F32)], axis=1)
    spread[d_me] = low.astype(BF16)
    for i in range(1, n_dp):
        c = pltpu.make_async_remote_copy(
            src_ref=spread.at[d_me],
            dst_ref=spread.at[d_me],
            send_sem=s_send.at[i],
            recv_sem=s_recv.at[d_me],
            device_id={"dp": lax.rem(d_me + i, n_dp)},
            device_id_type=MESH,
        )
        c.start()
        waits.append(c)

    loads[1].wait()
    gate_act = dot(x_in, gw_v[...])
    loads[2].wait()
    up_act = dot(x_in, uw_v[...])
    loads[3].wait()
    for i in range(n_dp):
        d = lax.rem(d_me + i, n_dp)
        if i:
            pltpu.make_async_copy(spread.at[d], spread.at[d], s_recv.at[d]).wait()
            pltpu.make_async_copy(expand.at[d], expand.at[d], x_recv.at[d]).wait()
        up_act += dot(spread[d][:, :pr], expand[d].reshape(pr, hidden_part))
    hidden = (gate_act / (1.0 + jnp.exp(-gate_act))) * up_act
    hid[d_me] = hidden.astype(BF16)
    for i in range(1, n_dp):
        c = pltpu.make_async_remote_copy(
            src_ref=hid.at[d_me],
            dst_ref=hid.at[d_me],
            send_sem=h_send.at[i],
            recv_sem=h_recv.at[d_me],
            device_id={"dp": lax.rem(d_me + i, n_dp)},
            device_id_type=MESH,
        )
        c.start()
        waits.append(c)

    j_col = iota((tokens, slots_out), 1)
    e_col = j_col // cap
    quant = gq[...]
    high = lax.shift_right_logical(quant, 8)
    rest = quant - high * 256
    assign = jnp.zeros((tokens, slots_out), F32)
    mix_high = jnp.zeros((tokens, slots_out), F32)
    mix_rest = jnp.zeros((tokens, slots_out), F32)
    for k in range(topk):
        hit = (routing[:, k : k + 1] == e_col).astype(F32)
        assign += hit
        mix_high += hit * (high[:, k : k + 1].astype(F32) * (256.0 / 32768.0))
        mix_rest += hit * (rest[:, k : k + 1].astype(F32) * (1.0 / 32768.0))
    lower = (iota((tokens, tokens), 1) < iota((tokens, tokens), 0)).astype(F32)
    rank = dot(lower, assign)
    here = (rank == lax.rem(j_col, cap).astype(F32)).astype(F32)
    mix = jnp.concatenate([mix_high * here, mix_rest * here], axis=0).astype(BF16)

    loads[4].wait()
    total = None
    for i in range(n_dp):
        d = lax.rem(d_me + i, n_dp)
        if i:
            pltpu.make_async_copy(hid.at[d], hid.at[d], h_recv.at[d]).wait()
        part = dot(
            hid[d], dw_v[pl.ds(pl.multiple_of(d * hidden_part, hidden_part), hidden_part), :]
        )
        total = part if total is None else total + part
    for z in range(n_e):
        for d in range(n_dp):
            base = (z * n_dp + d) * cap
            eout[z, d] = total[base : base + cap, :].astype(BF16)

    back[e_me, d_me] = eout[e_me, d_me]
    for i in sorted(range(n_e), key=lambda i: -min(i, n_e - i)):
        z = lax.rem(e_me + i, n_e)
        for j in range(n_dp - 1, -1, -1):
            if i == 0 and j == 0:
                continue
            d = lax.rem(d_me + j, n_dp)
            c = pltpu.make_async_remote_copy(
                src_ref=eout.at[z, d],
                dst_ref=back.at[e_me, d_me],
                send_sem=o_send.at[i, j],
                recv_sem=o_recv.at[e_me, d_me],
                device_id={"expert": z, "dp": d},
                device_id_type=MESH,
            )
            c.start()
            waits.append(c)
    for i in range(n_e):
        z = lax.rem(e_me + i, n_e)
        for j in range(n_dp):
            if i == 0 and j == 0:
                continue
            d = lax.rem(d_me + j, n_dp)
            pltpu.make_async_copy(back.at[z, d], back.at[z, d], o_recv.at[z, d]).wait()
    for d in range(n_dp):
        got = back[:, d].astype(F32).reshape(slots_out, out_part).astype(BF16)
        both = dot(mix, got)
        out[:, d * out_part : (d + 1) * out_part] = (both[:tokens] + both[tokens:]).astype(BF16)
    for c in waits:
        c.wait_send()


def per_device(n_e, n_dp, tok, rout, gq, ten, look, gw, uw, dw, shr, exp):
    tokens, width = tok.shape
    experts, tenants = look.shape
    cap = tokens // 4
    tail = -(-tenants // 128) * 128
    wide = width + tail
    pages, rank_dim = shr.shape[1:3]
    hidden_part = gw.shape[2]
    out_part = dw.shape[2]
    slot_count = n_e * n_dp * cap
    pr_pad = -(-pages * rank_dim // 128) * 128
    vmem = pl.BlockSpec(memory_space=pltpu.VMEM)
    hbm = pl.BlockSpec(memory_space=pl.ANY)
    dma = pltpu.SemaphoreType.DMA
    return pl.pallas_call(
        functools.partial(kernel, n_e, n_dp),
        out_shape=pltpu.VMEM((tokens, width), BF16),
        in_specs=[hbm] * 10,
        out_specs=vmem,
        scratch_shapes=[
            pltpu.VMEM((experts, cap, wide), BF16),
            pltpu.VMEM((n_e, n_dp, cap, wide), BF16),
            pltpu.VMEM((n_dp, slot_count, pr_pad), BF16),
            pltpu.VMEM((n_dp, pages, rank_dim, hidden_part), BF16),
            pltpu.VMEM((n_dp, slot_count, hidden_part), BF16),
            pltpu.VMEM((n_e, n_dp, cap, out_part), BF16),
            pltpu.VMEM((n_e, n_dp, cap, out_part), BF16),
            pltpu.VMEM(gw.shape[1:], BF16),
            pltpu.VMEM(uw.shape[1:], BF16),
            pltpu.VMEM(dw.shape[1:], BF16),
            pltpu.VMEM(shr.shape[1:], BF16),
            pltpu.VMEM(tok.shape, BF16),
            pltpu.VMEM(rout.shape, jnp.int32),
            pltpu.VMEM(gq.shape, jnp.int32),
            pltpu.SMEM(ten.shape, jnp.int32),
            pltpu.VMEM(look.shape, jnp.int32),
            dma((5,)),
            dma((5,)),
            dma((n_e,)),
            dma((n_e, n_dp)),
            dma((n_e, n_dp)),
            dma((n_dp,)),
            dma((n_dp,)),
            dma((n_dp,)),
            dma((n_dp,)),
            dma((n_dp,)),
            dma((n_dp,)),
            dma((n_e, n_dp)),
            dma((n_e, n_dp)),
        ],
        compiler_params=pltpu.CompilerParams(collective_id=0, has_side_effects=True),
    )(tok, rout, gq, ten, look, gw, uw, dw, shr, exp)


def solution(mesh):
    return jax.shard_map(
        functools.partial(per_device, mesh.shape["expert"], mesh.shape["dp"]),
        mesh=mesh,
        in_specs=(
            P(("group", "expert", "dp"), None),
            P(("group", "expert", "dp"), None),
            P(("group", "expert", "dp"), None),
            P(("group", "expert", "dp")),
            P(),
            P("expert", None, "dp"),
            P("expert", None, "dp"),
            P("expert", None, "dp"),
            P("expert", "dp", None, None),
            P("expert", "dp", None, None),
        ),
        out_specs=P(("group", "expert", "dp"), None),
        check_vma=False,
    )
```

```python
import functools

import jax
import jax.numpy as jnp
from jax import lax
from jax.experimental import pallas as pl
from jax.experimental.pallas import tpu as pltpu
from jax.sharding import PartitionSpec as P

MESH = pl.DeviceIdType.MESH
F32 = jnp.float32
BF16 = jnp.bfloat16


def iota(shape, dim):
    return lax.broadcasted_iota(jnp.int32, shape, dim)


def near(e, k, n):
    low = jnp.minimum(e, n - 1 - e)
    pair = e - (k + 1) // 2 if k % 2 else e + k // 2
    rest = jnp.where(2 * e < n - 1, k, n - 1 - k)
    return jnp.where(k <= 2 * low, pair, rest)


def far_first(n):
    return sorted(range(1, n), key=lambda i: abs(i - n // 2))


def dot(a, b):
    return jnp.dot(a, b, preferred_element_type=F32)


def dot_nt(a, b):
    return lax.dot_general(a, b, (((1,), (1,)), ((), ())), preferred_element_type=F32)


def kernel(
    n_e,
    n_dp,
    tok_h,
    rout_h,
    gq_h,
    ten_h,
    look_h,
    gw,
    uw,
    dw,
    shr,
    exp,
    out,
    send,
    rows,
    spread,
    expand,
    hid,
    eout,
    back,
    gw_v,
    uw_v,
    dw_v,
    shr_v,
    tok,
    rout,
    gq,
    ten,
    look,
    small_sem,
    load_sem,
    z_send,
    row_recv,
    f_send,
    x_send,
    x_recv,
    s_send,
    s_recv,
    h_send,
    h_recv,
    o_send,
    o_recv,
):
    e_me = lax.axis_index("expert")
    d_me = lax.axis_index("dp")
    tokens, width = tok.shape
    experts, tenants = look.shape
    topk = rout.shape[1]
    cap = send.shape[1]
    slots_out = experts * cap
    wide = send.shape[2]
    pages, rank_dim = shr_v.shape[:2]
    hidden_part = gw_v.shape[1]
    out_part = dw_v.shape[1]
    pr = pages * rank_dim

    barrier = pltpu.get_barrier_semaphore()
    for i in range(1, n_e):
        pl.semaphore_signal(
            barrier, inc=1, device_id={"expert": lax.rem(e_me + i, n_e)}, device_id_type=MESH
        )
    for i in range(1, n_dp):
        pl.semaphore_signal(
            barrier, inc=1, device_id={"dp": lax.rem(d_me + i, n_dp)}, device_id_type=MESH
        )

    small = [
        pltpu.make_async_copy(src, dst, small_sem.at[i])
        for i, (src, dst) in enumerate(
            ((rout_h, rout), (ten_h, ten), (look_h, look), (tok_h, tok), (gq_h, gq))
        )
    ]
    for c in small:
        c.start()
    loads = [
        pltpu.make_async_copy(shr.at[0], shr_v, load_sem.at[0]),
        pltpu.make_async_copy(gw.at[0], gw_v, load_sem.at[1]),
        pltpu.make_async_copy(uw.at[0], uw_v, load_sem.at[2]),
        pltpu.make_async_copy(
            exp.at[0, :, :, pl.ds(pl.multiple_of(d_me * hidden_part, hidden_part), hidden_part)],
            expand.at[d_me],
            load_sem.at[3],
        ),
        pltpu.make_async_copy(dw.at[0], dw_v, load_sem.at[4]),
    ]
    for c in loads:
        c.start()

    for c in small:
        c.wait()
    routing = rout[...]
    routing_f = routing.astype(F32)
    eye = (iota((topk, topk), 0) == iota((topk, topk), 1)).astype(F32)
    routing_t = dot_nt(eye, routing_f)
    j_row = iota((slots_out, tokens), 0)
    e_row = (j_row // cap).astype(F32)
    assign_t = jnp.zeros((slots_out, tokens), F32)
    for k in range(topk):
        assign_t += (routing_t[k : k + 1, :] == e_row).astype(F32)
    upper = (iota((tokens, tokens), 0) < iota((tokens, tokens), 1)).astype(F32)
    rank_t = dot(assign_t, upper)
    place_t = assign_t * (rank_t == lax.rem(j_row, cap).astype(F32)).astype(F32)
    x_out = dot(place_t.astype(BF16), tok[...])
    ten_row = iota((tokens, tenants), 0)
    ten_col = jnp.zeros((tokens, tenants), jnp.int32)
    for t in range(tokens):
        ten_col = jnp.where(ten_row == t, ten[t], ten_col)
    ten_hot = (ten_col == iota((tokens, tenants), 1)).astype(F32)
    slot_ten = dot(place_t, ten_hot)
    pick_e = (iota((slots_out, experts), 0) // cap == iota((slots_out, experts), 1)).astype(F32)
    look_rows = dot(pick_e, look[...].astype(F32))
    page = jnp.sum(slot_ten * look_rows, axis=1, keepdims=True)
    filled = jnp.sum(slot_ten, axis=1, keepdims=True)
    tail = wide - width
    page_hot = (page == iota((slots_out, tail), 1).astype(F32)).astype(F32) * filled
    for e in range(experts):
        send[e, :, :width] = x_out[e * cap : (e + 1) * cap, :].astype(BF16)
        send[e, :, width:] = page_hot[e * cap : (e + 1) * cap, :].astype(BF16)
    rows[e_me, d_me] = send[e_me]

    pl.semaphore_wait(barrier, n_e - 1 + n_dp - 1)

    waits = []
    order = sorted(range(1, n_e), key=lambda i: -min(i, n_e - i))
    for i in order:
        e = lax.rem(e_me + i, n_e)
        c = pltpu.make_async_remote_copy(
            src_ref=send.at[e],
            dst_ref=rows.at[e_me, d_me],
            send_sem=z_send.at[i],
            recv_sem=row_recv.at[e_me, d_me],
            device_id={"expert": e},
            device_id_type=MESH,
        )
        c.start()
        waits.append(c)

    def forward(z, slot):
        for i in range(1, n_dp):
            c = pltpu.make_async_remote_copy(
                src_ref=rows.at[z, d_me],
                dst_ref=rows.at[z, d_me],
                send_sem=f_send.at[slot, i],
                recv_sem=row_recv.at[z, d_me],
                device_id={"dp": lax.rem(d_me + i, n_dp)},
                device_id_type=MESH,
            )
            c.start()
            waits.append(c)

    def row_wait(z, d):
        pltpu.make_async_copy(rows.at[z, d], rows.at[z, d], row_recv.at[z, d]).wait()

    forward(e_me, 0)
    for i in range(1, n_dp):
        d = lax.rem(d_me + i, n_dp)
        c = pltpu.make_async_remote_copy(
            src_ref=exp.at[
                0, :, :, pl.ds(pl.multiple_of(d * hidden_part, hidden_part), hidden_part)
            ],
            dst_ref=expand.at[d_me],
            send_sem=x_send.at[i],
            recv_sem=x_recv.at[d_me],
            device_id={"dp": d},
            device_id_type=MESH,
        )
        c.start()
        waits.append(c)
    for i in sorted(range(1, n_e), key=lambda i: min(i, n_e - i)):
        z = lax.rem(e_me + i, n_e)
        row_wait(z, d_me)
        forward(z, i)
    for i in range(1, n_dp):
        for z in range(n_e):
            row_wait(z, lax.rem(d_me + i, n_dp))

    slot_count = n_e * n_dp * cap
    x_all = rows[...].astype(F32).reshape(slot_count, wide).astype(BF16)
    x_in = x_all[:, :width]
    hot = x_all[:, width:]
    loads[0].wait()
    products = dot_nt(x_in, shr_v[...].reshape(pr, width))
    own_pages = (
        iota((tail, pr), 0) == d_me * pages + iota((tail, pr), 1) // rank_dim
    ).astype(BF16)
    mask = dot(hot, own_pages)
    pad = spread.shape[2] - pr
    low = products.astype(BF16).astype(F32) * mask
    if pad:
        low = jnp.concatenate([low, jnp.zeros((slot_count, pad), F32)], axis=1)
    spread[d_me] = low.astype(BF16)
    for i in range(1, n_dp):
        c = pltpu.make_async_remote_copy(
            src_ref=spread.at[d_me],
            dst_ref=spread.at[d_me],
            send_sem=s_send.at[i],
            recv_sem=s_recv.at[d_me],
            device_id={"dp": lax.rem(d_me + i, n_dp)},
            device_id_type=MESH,
        )
        c.start()
        waits.append(c)

    loads[1].wait()
    gate_act = dot(x_in, gw_v[...])
    loads[2].wait()
    up_act = dot(x_in, uw_v[...])
    loads[3].wait()
    for i in range(n_dp):
        d = lax.rem(d_me + i, n_dp)
        if i:
            pltpu.make_async_copy(spread.at[d], spread.at[d], s_recv.at[d]).wait()
            pltpu.make_async_copy(expand.at[d], expand.at[d], x_recv.at[d]).wait()
        up_act += dot(spread[d][:, :pr], expand[d].reshape(pr, hidden_part))
    hidden = (gate_act / (1.0 + jnp.exp(-gate_act))) * up_act
    hid[d_me] = hidden.astype(BF16)
    for i in range(1, n_dp):
        c = pltpu.make_async_remote_copy(
            src_ref=hid.at[d_me],
            dst_ref=hid.at[d_me],
            send_sem=h_send.at[i],
            recv_sem=h_recv.at[d_me],
            device_id={"dp": lax.rem(d_me + i, n_dp)},
            device_id_type=MESH,
        )
        c.start()
        waits.append(c)

    j_col = iota((tokens, slots_out), 1)
    e_col = j_col // cap
    quant = gq[...]
    high = lax.shift_right_logical(quant, 8)
    rest = quant - high * 256
    assign = jnp.zeros((tokens, slots_out), F32)
    mix_high = jnp.zeros((tokens, slots_out), F32)
    mix_rest = jnp.zeros((tokens, slots_out), F32)
    for k in range(topk):
        hit = (routing[:, k : k + 1] == e_col).astype(F32)
        assign += hit
        mix_high += hit * (high[:, k : k + 1].astype(F32) * (256.0 / 32768.0))
        mix_rest += hit * (rest[:, k : k + 1].astype(F32) * (1.0 / 32768.0))
    lower = (iota((tokens, tokens), 1) < iota((tokens, tokens), 0)).astype(F32)
    rank = dot(lower, assign)
    here = (rank == lax.rem(j_col, cap).astype(F32)).astype(F32)
    mix = jnp.concatenate([mix_high * here, mix_rest * here], axis=0).astype(BF16)

    loads[4].wait()
    total = None
    for i in range(n_dp):
        d = lax.rem(d_me + i, n_dp)
        if i:
            pltpu.make_async_copy(hid.at[d], hid.at[d], h_recv.at[d]).wait()
        part = dot(
            hid[d], dw_v[pl.ds(pl.multiple_of(d * hidden_part, hidden_part), hidden_part), :]
        )
        total = part if total is None else total + part
    for z in range(n_e):
        for d in range(n_dp):
            base = (z * n_dp + d) * cap
            eout[z, d] = total[base : base + cap, :].astype(BF16)

    back[e_me, d_me] = eout[e_me, d_me]
    for i in range(n_e - 1, -1, -1):
        z = near(e_me, i, n_e)
        for j in range(n_dp - 1, -1, -1):
            if i == 0 and j == 0:
                continue
            d = lax.rem(d_me + j, n_dp)
            c = pltpu.make_async_remote_copy(
                src_ref=eout.at[z, d],
                dst_ref=back.at[e_me, d_me],
                send_sem=o_send.at[i, j],
                recv_sem=o_recv.at[e_me, d_me],
                device_id={"expert": z, "dp": d},
                device_id_type=MESH,
            )
            c.start()
            waits.append(c)
    for i in range(n_e):
        z = lax.rem(e_me + i, n_e)
        for j in range(n_dp):
            if i == 0 and j == 0:
                continue
            d = lax.rem(d_me + j, n_dp)
            pltpu.make_async_copy(back.at[z, d], back.at[z, d], o_recv.at[z, d]).wait()
    for d in range(n_dp):
        got = back[:, d].astype(F32).reshape(slots_out, out_part).astype(BF16)
        both = dot(mix, got)
        out[:, d * out_part : (d + 1) * out_part] = (both[:tokens] + both[tokens:]).astype(BF16)
    for c in waits:
        c.wait_send()


def per_device(n_e, n_dp, tok, rout, gq, ten, look, gw, uw, dw, shr, exp):
    tokens, width = tok.shape
    experts, tenants = look.shape
    cap = tokens // 4
    tail = -(-tenants // 128) * 128
    wide = width + tail
    pages, rank_dim = shr.shape[1:3]
    hidden_part = gw.shape[2]
    out_part = dw.shape[2]
    slot_count = n_e * n_dp * cap
    pr_pad = -(-pages * rank_dim // 128) * 128
    vmem = pl.BlockSpec(memory_space=pltpu.VMEM)
    hbm = pl.BlockSpec(memory_space=pl.ANY)
    dma = pltpu.SemaphoreType.DMA
    return pl.pallas_call(
        functools.partial(kernel, n_e, n_dp),
        out_shape=pltpu.VMEM((tokens, width), BF16),
        in_specs=[hbm] * 10,
        out_specs=vmem,
        scratch_shapes=[
            pltpu.VMEM((experts, cap, wide), BF16),
            pltpu.VMEM((n_e, n_dp, cap, wide), BF16),
            pltpu.VMEM((n_dp, slot_count, pr_pad), BF16),
            pltpu.VMEM((n_dp, pages, rank_dim, hidden_part), BF16),
            pltpu.VMEM((n_dp, slot_count, hidden_part), BF16),
            pltpu.VMEM((n_e, n_dp, cap, out_part), BF16),
            pltpu.VMEM((n_e, n_dp, cap, out_part), BF16),
            pltpu.VMEM(gw.shape[1:], BF16),
            pltpu.VMEM(uw.shape[1:], BF16),
            pltpu.VMEM(dw.shape[1:], BF16),
            pltpu.VMEM(shr.shape[1:], BF16),
            pltpu.VMEM(tok.shape, BF16),
            pltpu.VMEM(rout.shape, jnp.int32),
            pltpu.VMEM(gq.shape, jnp.int32),
            pltpu.SMEM(ten.shape, jnp.int32),
            pltpu.VMEM(look.shape, jnp.int32),
            dma((5,)),
            dma((5,)),
            dma((n_e,)),
            dma((n_e, n_dp)),
            dma((n_e, n_dp)),
            dma((n_dp,)),
            dma((n_dp,)),
            dma((n_dp,)),
            dma((n_dp,)),
            dma((n_dp,)),
            dma((n_dp,)),
            dma((n_e, n_dp)),
            dma((n_e, n_dp)),
        ],
        compiler_params=pltpu.CompilerParams(collective_id=0, has_side_effects=True),
    )(tok, rout, gq, ten, look, gw, uw, dw, shr, exp)


def solution(mesh):
    return jax.shard_map(
        functools.partial(per_device, mesh.shape["expert"], mesh.shape["dp"]),
        mesh=mesh,
        in_specs=(
            P(("group", "expert", "dp"), None),
            P(("group", "expert", "dp"), None),
            P(("group", "expert", "dp"), None),
            P(("group", "expert", "dp")),
            P(),
            P("expert", None, "dp"),
            P("expert", None, "dp"),
            P("expert", None, "dp"),
            P("expert", "dp", None, None),
            P("expert", "dp", None, None),
        ),
        out_specs=P(("group", "expert", "dp"), None),
        check_vma=False,
    )
```
